512 devices in a mesh: rep: 64 (over x, y, core), tp: 8 (over z).
Axes of the slice: x: 4, y: 8, z: 8, core: 2. Of those that a mesh axis runs over, the one named last changes fastest.
Arguments:
- tokens: bfloat16 [16384, 8192], P('rep', 'tp'), may hold values from -6 to 6
- key_weight_base: bfloat16 [8192, 1024], P('tp'), may hold values from -0.0625 to 0.0625
- adapter_down_maps: bfloat16 [64, 8192, 64], P('rep', 'tp'), may hold values from -0.0625 to 0.0625
- adapter_up_maps: bfloat16 [64, 64, 1024], P('rep', None, 'tp'), may hold values from -0.75 to 0.75
- adapter_index: int32 [64, 256], P('rep'), may hold values from 0 to 63, never falling along the last dimension, each value on 1 to 8 neighbouring positions
- plan: int32 [16384, 1], P('rep'), may hold values from 0 to 63; in each aligned block of 256 rows (0 to 255, 256 to 511, ...) at most 8 rows name the same one
Outputs:
- keys_out: bfloat16 [32768, 1024], P('rep', 'tp')
The draws below stay inside these ranges and needn't reach their ends.
Inputs may be any that keep to these rules, and one draw needn't show every extreme that they name: `adapter_index`: each replica's rows are ordered by adapter; at most 8 rows of one replica use one adapter, and some replica reaches it. `plan`: at most 8 rows of one replica have one destination, and some replica reaches it.
All inputs are finite; a program needn't handle non-finite values.
Results may differ from the reference program's by a relative error of at most 0.0045.
Values may be sent and summed in bfloat16 or wider, within the bound.
A program may use at most 64 MiB of HBM per device.

```python
import math
import jax
import jax.numpy as jnp
import numpy as np
from jax import lax

MODEL_WIDTH = 8192
ADAPTER_RANK = 64
ROW_DEV = 256
KEY_FEATURES = 1024
ADAPTER_COUNT = 64
SEG_MOST = 8
CAP_MOVE = 8
ROWS = 16384
N_REP = 64


def block_levels(stream_key, extent, split, smallest, high):
    loudness, own = 1.0, jax.random.fold_in(stream_key, 6)
    for position, parts in split:
        steps = jnp.exp(jax.random.uniform(jax.random.fold_in(own, position), (parts,), jnp.float32, smallest / len(split), high / len(split)))
        loudness = loudness * jnp.repeat(steps, extent[position] // parts).reshape([-1 if axis == position else 1 for axis in range(len(extent))])
    return loudness


def split_up(count, total, reach, skew):
    weights = [(1 << 20) // math.isqrt(grade ** skew) + 1 for grade in range(2, count + 1)]
    rest, given = total - reach - (count - 1), [1] * (count - 1)
    while rest > 0:
        movable = [i for i in range(count - 1) if given[i] < reach]
        whole, left = sum([weights[i] for i in movable]), rest
        for i in movable:
            addition = min(reach - given[i], max(1, left * weights[i] // whole), rest)
            given[i] = given[i] + addition
            rest = rest - addition
    return np.array([reach] + given)


def ragged_sizes(rng, count, total, limit, skew):
    if count == 2:
        one = jax.random.randint(rng, (), max(1, total - limit), min(limit, total - 1) + 1)
        return jnp.stack([one, total - one])
    sizes = jnp.asarray(split_up(count, total, limit, skew), jnp.int32)
    twos = (count - 1) // 2
    donor, taker = sizes[1:1 + 2 * twos:2], sizes[2:2 + 2 * twos:2]
    slack = jnp.minimum(donor - 1, limit - taker)
    moved = jax.random.randint(jax.random.fold_in(rng, 1), (twos,), 0, 1 << 20) % (slack + 1)
    sizes = sizes.at[1:1 + 2 * twos:2].set(donor - moved).at[2:2 + 2 * twos:2].set(taker + moved)
    return sizes[jax.random.permutation(jax.random.fold_in(rng, 2), count)]


def shared_out(own_key, own, number, rows, count, top, bound, lean):
    ranking = jax.random.permutation(own_key, count)
    crowded, usual = portions_of(count, rows * top, bound, lean, True), portions_of(count, rows * top, bound, lean, False)
    places = jnp.arange(count)

    def named(sizes, offset_by):
        used = int((sizes > 0).sum())
        fixed = max(1, used // 4)
        moved = fixed + (places - fixed + offset_by * (used - fixed)) % max(1, count - fixed)
        return jnp.zeros((count,), jnp.int32).at[ranking[jnp.where(places < fixed, places, moved)]].set(jnp.asarray(sizes, jnp.int32))

    sizes = jnp.where(number % 4 == 0, named(crowded, number // 4), named(usual, number - number // 4 - 1))
    mixed = jax.random.permutation(jax.random.fold_in(own, 3), count)
    giver, taker = mixed[0:count // 2 * 2:2], mixed[1:count // 2 * 2:2]
    room = jnp.minimum(sizes[giver] - 1, bound - sizes[taker]) // 2
    room = jnp.where((giver == ranking[0]) | (taker == ranking[0]) | (sizes[taker] == 0), 0, jnp.maximum(room, 0))
    moved = jax.random.randint(jax.random.fold_in(own, 4), (count // 2,), 0, 1 << 20) % (room + 1)
    sizes = sizes.at[giver].add(-moved).at[taker].add(moved)
    items = jnp.searchsorted(jnp.cumsum(sizes), jnp.arange(rows * top), side="right").astype(jnp.int32)
    table = items.reshape(top, rows).T
    table = table[jax.random.permutation(jax.random.fold_in(own, 1), rows)]
    offset_by = jax.random.randint(jax.random.fold_in(own, 2), (rows, 1), 0, top)
    return jnp.take_along_axis(table, (jnp.arange(top)[None, :] + offset_by) % top, axis=1)


def portions_of(amount, total, reach, slope, full):
    weights = [(1 << 20) // math.isqrt(rank ** slope) + 1 for rank in range(1, amount + 1)]
    largest = reach if full else min(reach, max(-(-total // amount), total * weights[0] // sum(weights)))
    least = 1 if total - largest >= amount - 1 else 0
    given, rest = [largest] + [least] * (amount - 1), total - largest - least * (amount - 1)
    while rest > 0:
        candidates = [i for i in range(1, amount) if given[i] < largest] or [i for i in range(1, amount) if given[i] < reach]
        mass, remaining = sum([weights[i] for i in candidates]), rest
        for i in candidates:
            extra = min(reach - given[i], max(1, remaining * weights[i] // mass), rest)
            given[i] = given[i] + extra
            rest = rest - extra
    return np.array(given)


def gaussian(rng, dims, scale, most, pieces=(), kind=jnp.bfloat16):
    result = scale * jax.random.normal(rng, dims, jnp.float32)
    if pieces:
        result = result * block_levels(rng, dims, pieces, -0.22, 0.18)
    return jnp.clip(result, -most, most).astype(kind)


def setup_inputs(seed: int = 0) -> dict:
    seeds = jax.random.split(jax.random.key(seed), 7)
    tokens = gaussian(seeds[0], (ROWS, MODEL_WIDTH), 1.0, 6.0, ((0, 64), (1, 8)))
    key_weight_base = gaussian(seeds[1], (MODEL_WIDTH, KEY_FEATURES), MODEL_WIDTH ** -0.5, 0.0625, ((0, 8),))
    adapter_down_maps = gaussian(seeds[2], (ADAPTER_COUNT, MODEL_WIDTH, ADAPTER_RANK), MODEL_WIDTH ** -0.5, 0.0625, ((0, 64), (1, 8)))
    adapter_up_maps = gaussian(seeds[3], (ADAPTER_COUNT, ADAPTER_RANK, KEY_FEATURES), ADAPTER_RANK ** -0.5, 0.75, ((0, 64), (2, 8)))
    adapter_index = jax.vmap(lambda own: jnp.searchsorted(jnp.cumsum(ragged_sizes(own, ADAPTER_COUNT, ROW_DEV, SEG_MOST, 2)), jnp.arange(ROW_DEV), side="right"))(jax.random.split(seeds[4], N_REP)).reshape((N_REP, ROW_DEV)).astype(jnp.int32)
    plan_keys = jax.random.split(jax.random.fold_in(seeds[5], 1), ROWS // ROW_DEV)
    plan_turns = jax.random.permutation(jax.random.fold_in(seeds[5], 3), ROWS // ROW_DEV)
    plan = jax.vmap(lambda own, number: shared_out(jax.random.fold_in(seeds[5], 2), own, number, ROW_DEV, N_REP, 1, CAP_MOVE, 2))(plan_keys, plan_turns).reshape((ROWS, 1))
    return dict(tokens=tokens, key_weight_base=key_weight_base, adapter_down_maps=adapter_down_maps, adapter_up_maps=adapter_up_maps, adapter_index=adapter_index, plan=plan)


def reference(tokens, key_weight_base, adapter_down_maps, adapter_up_maps, adapter_index, plan):
    x_all = tokens.reshape(N_REP, ROW_DEV, MODEL_WIDTH)
    dest_all = plan.reshape(N_REP, ROW_DEV)
    down_factor = adapter_down_maps.astype(jnp.float32)
    up_factor = adapter_up_maps.astype(jnp.float32)
    adapter_range = jnp.arange(ADAPTER_COUNT, dtype=jnp.int32)
    slot_range = jnp.arange(SEG_MOST, dtype=jnp.int32)
    row_range = jnp.arange(ROW_DEV, dtype=jnp.int32)
    dest_range = jnp.arange(N_REP, dtype=jnp.int32)

    def per_source(items):
        x_rows, ids, dest = items
        base = jnp.dot(x_rows, key_weight_base, preferred_element_type=jnp.float32)
        starts = jnp.sum((ids[None, :] < adapter_range[:, None]).astype(jnp.int32), axis=1).astype(jnp.int32)
        counts = jnp.sum((ids[None, :] == adapter_range[:, None]).astype(jnp.int32), axis=1).astype(jnp.int32)
        index = jnp.clip(starts[:, None] + slot_range[None, :], 0, ROW_DEV - 1).astype(jnp.int32)
        valid = slot_range[None, :] < counts[:, None]
        packed = jnp.where(valid[:, :, None], x_rows[index], jnp.zeros((), x_rows.dtype))
        upart = jnp.einsum("asd,adr->asr", packed.astype(jnp.float32), down_factor)
        u_low = upart.astype(jnp.bfloat16)
        delta = jnp.einsum("asr,ark->ask", u_low.astype(jnp.float32), up_factor)
        flat = (ids * SEG_MOST + row_range - starts[ids]).astype(jnp.int32)
        row_delta = delta.reshape(ADAPTER_COUNT * SEG_MOST, KEY_FEATURES)[flat]
        keyrow = (base + 2.0 * row_delta).astype(jnp.bfloat16)
        onehot = (dest[:, None] == dest_range[None, :]).astype(jnp.int32)
        before = jnp.cumsum(onehot, axis=0, dtype=jnp.int32) - onehot
        slot = jnp.sum(before * onehot, axis=1).astype(jnp.int32)
        buffer = jnp.zeros((N_REP, CAP_MOVE, KEY_FEATURES), jnp.bfloat16).at[dest, slot].set(keyrow)
        return buffer

    buffers = lax.map(per_source, (x_all, adapter_index, dest_all))
    return jnp.transpose(buffers, (1, 0, 2, 3)).reshape(N_REP * N_REP * CAP_MOVE, KEY_FEATURES)
```

```python
import jax
import jax.numpy as jnp
from jax import lax
from jax.experimental import pallas as pl
from jax.experimental.pallas import tpu as pltpu
from jax.sharding import PartitionSpec as P

MESH = pl.DeviceIdType.MESH
F32 = jnp.float32
BF16 = jnp.bfloat16
NX, NY, NC, NZ = 4, 8, 2, 8
REP = NX * NY * NC
GRP = NX * NC
ROWS = 256
WIDTH = 1024
KEYS = 1024
RANK = 64
PART = 128
SLOTS = 8
PACK = REP * SLOTS


def iota(shape, dim):
    return lax.broadcasted_iota(jnp.int32, shape, dim)


def onehot(cond):
    return jnp.where(cond, 1.0, 0.0).astype(BF16)


def kernel(
    tok, w, down, up, ids, dest, out,
    psend, rrecv, dbuf, ubuf, bsend, brecv, csend, crecv, usend, urecv, dsend, drecv, osend, orecv, keyrow,
    s_x, r_x, s_yr, r_yr, s_yl, r_yl, s_ur, r_ur, s_ul, r_ul, s_b, r_b, s_c, r_c, s_u, r_u, s_d, r_d, s_o, r_o,
):
    me = lax.axis_index("rep")
    z = lax.axis_index("tp")
    mx = me // (NY * NC)
    my = (me // NC) % NY
    mc = me % NC
    mh = mx * NC + mc

    def rep_of(h, y):
        return ((h // NC) * NY + y) * NC + h % NC

    def grp(k):
        return (mh + k) % GRP

    def zp(k):
        return (z + k) % NZ

    barrier = pltpu.get_barrier_semaphore()

    def greet_rep(k, c):
        pl.semaphore_signal(barrier, inc=1, device_id={"rep": (me + k) % REP}, device_id_type=MESH)
        return c

    def greet_z(k, c):
        pl.semaphore_signal(barrier, inc=1, device_id={"tp": zp(k)}, device_id_type=MESH)
        return c

    lax.fori_loop(1, REP, greet_rep, 0)
    lax.fori_loop(1, NZ, greet_z, 0)

    eye = onehot(iota((RANK, RANK), 0) == iota((RANK, RANK), 1))
    dbuf[my] = lax.dot_general(eye, down[...], (((1,), (1,)), ((), ())), preferred_element_type=F32).astype(BF16)
    ubuf[my] = up[...]

    a = ids[...]
    lane = iota((1, ROWS), 1)
    rank = jnp.zeros((1, ROWS), jnp.int32)
    for k in range(1, SLOTS):
        rank = rank + jnp.where((lane >= k) & (pltpu.roll(a, k, 1) == a), 1, 0)
    ay = (a // NC) % NY
    spot = ((a // (NY * NC)) * NC + a % NC) * (NY * SLOTS) + (ay % 2) * 32 + (ay // 2) * SLOTS + rank
    pick = onehot(iota((PACK, ROWS), 0) == spot)
    for t in range(4):
        cols = slice(256 * t, 256 * t + 256)
        got = jnp.dot(pick, tok[:, cols], preferred_element_type=F32)
        psend[:, :, cols] = got.reshape(GRP, PACK // GRP, 256).astype(BF16)

    pl.semaphore_wait(barrier, REP - 1 + NZ - 1)

    right = rep_of(mh, (my + 1) % NY)
    left = rep_of(mh, (my + NY - 1) % NY)

    def ring(buf, ss, rs, s, to, step):
        i = (my + NY + step * s) % NY
        return pltpu.make_async_remote_copy(
            src_ref=buf.at[i], dst_ref=buf.at[i], send_sem=ss.at[s], recv_sem=rs.at[s],
            device_id={"rep": to}, device_id_type=MESH)

    to_right = [(ring(dbuf, s_yr, r_yr, s, right, -1), ring(ubuf, s_ur, r_ur, s, right, -1)) for s in range(4)]
    to_left = [(ring(dbuf, s_yl, r_yl, s, left, 1), ring(ubuf, s_ul, r_ul, s, left, 1)) for s in range(3)]
    for c in to_right[0] + to_left[0]:
        c.start()

    def xcopy(k):
        h = grp(k)
        return pltpu.make_async_remote_copy(
            src_ref=psend.at[h], dst_ref=rrecv.at[mh], send_sem=s_x.at[k], recv_sem=r_x.at[k],
            device_id={"rep": rep_of(h, my)}, device_id_type=MESH)

    def run(make, what, count):
        def body(k, c):
            getattr(make(k), what)()
            return c
        lax.fori_loop(1, count, body, 0)

    run(xcopy, "start", GRP)
    rrecv[mh] = psend[mh]

    for t in range(4):
        got = jnp.dot(tok[...], w[:, 256 * t:256 * t + 256], preferred_element_type=F32).astype(BF16)
        bsend[2 * t] = got[:, :PART]
        bsend[2 * t + 1] = got[:, PART:]

    def zcopy(src, dst, ss, rs):
        def make(k):
            return pltpu.make_async_remote_copy(
                src_ref=src(zp(k)), dst_ref=dst.at[z], send_sem=ss.at[k], recv_sem=rs.at[k],
                device_id={"tp": zp(k)}, device_id_type=MESH)
        return make

    bcopy = zcopy(lambda t: bsend.at[t], brecv, s_b, r_b)
    run(bcopy, "start", NZ)
    brecv[z] = bsend[z]

    square = iota((ROWS, ROWS), 0) == iota((ROWS, ROWS), 1)
    spot_col = jnp.sum(jnp.where(square, spot.astype(F32), 0.0), axis=1, keepdims=True).astype(jnp.int32)
    back = onehot(iota((ROWS, PACK), 1) == spot_col)
    d_col = dest[...]
    d_row = jnp.sum(jnp.where(square, d_col.astype(F32), 0.0), axis=0, keepdims=True).astype(jnp.int32)
    earlier = (d_col == d_row) & (iota((ROWS, ROWS), 0) < iota((ROWS, ROWS), 1))
    slot = jnp.sum(jnp.where(earlier, 1.0, 0.0), axis=0, keepdims=True).astype(jnp.int32)
    place = onehot(iota((PACK, ROWS), 0) == d_row * SLOTS + slot)

    for s in range(1, 4):
        for c in to_right[s - 1]:
            c.wait_recv()
        for c in to_right[s]:
            c.start()
        for c in to_left[s - 1]:
            c.wait_recv()
        if s < 3:
            for c in to_left[s]:
                c.start()
    for c in to_right[3]:
        c.wait_recv()
    run(xcopy, "wait_recv", GRP)

    r_all = rrecv[...].reshape(PACK, WIDTH)
    fold = jnp.zeros((PACK, PART), F32)
    row = iota((PACK, PART), 0)
    half = iota((PACK, PART), 1) // RANK
    mine = (row % 64) // 32 == half
    for t in range(2):
        d4 = dbuf[4 * t:4 * t + 4].reshape(4 * RANK, WIDTH)
        got = lax.dot_general(r_all, d4, (((1,), (1,)), ((), ())), preferred_element_type=F32)
        for i in range(2):
            keep = mine & ((row % 32) // SLOTS == 2 * t + i)
            fold = fold + jnp.where(keep, got[:, PART * i:PART * i + PART], 0.0)
    fold = fold.reshape(GRP, 2, 32, PART)
    csend[...] = fold[:, 0] + fold[:, 1]
    ccopy = zcopy(lambda t: csend.at[t], crecv, s_c, r_c)
    run(ccopy, "start", NZ)
    crecv[z] = csend[z]
    run(bcopy, "wait_recv", NZ)
    base = jnp.sum(brecv[...].astype(F32), axis=0)
    run(ccopy, "wait_recv", NZ)
    usend[...] = jnp.sum(crecv[...], axis=0).astype(BF16)
    ucopy = zcopy(lambda t: usend, urecv, s_u, r_u)
    run(ucopy, "start", NZ)
    urecv[z] = usend[...]
    run(ucopy, "wait_recv", NZ)

    u = urecv[...].reshape(PACK // 2, PART)
    row2 = iota((PACK // 2, PART), 0)
    half2 = iota((PACK // 2, PART), 1) // RANK
    u_all = ubuf[...].reshape(NY * RANK, PART)
    zero = jnp.zeros((), BF16)
    for p in range(2):
        wide = jnp.concatenate(
            [jnp.where(((row2 % 32) // SLOTS == i) & (half2 == p), u, zero) for i in range(4)], axis=1)
        got = jnp.dot(wide, u_all, preferred_element_type=F32)
        dsend[:, 32 * p:32 * p + 32] = got.reshape(GRP, 32, PART).astype(BF16)

    def dcopy(k):
        h = grp(k)
        return pltpu.make_async_remote_copy(
            src_ref=dsend.at[h], dst_ref=drecv.at[mh], send_sem=s_d.at[k], recv_sem=r_d.at[k],
            device_id={"rep": rep_of(h, my)}, device_id_type=MESH)

    run(dcopy, "start", GRP)
    drecv[mh] = dsend[mh]
    run(dcopy, "wait_recv", GRP)

    delta = jnp.dot(back, drecv[...].reshape(PACK, PART), preferred_element_type=F32)
    keyrow[...] = (base + 2.0 * delta).astype(BF16)
    got = jnp.dot(place, keyrow[...], preferred_element_type=F32)
    osend[...] = got.reshape(REP, SLOTS, PART).astype(BF16)

    def ocopy(k):
        to = (me + k) % REP
        return pltpu.make_async_remote_copy(
            src_ref=osend.at[to], dst_ref=orecv.at[me], send_sem=s_o.at[k], recv_sem=r_o.at[k],
            device_id={"rep": to}, device_id_type=MESH)

    run(ocopy, "start", REP)
    orecv[me] = osend[me]
    for pair in to_right + to_left:
        for c in pair:
            c.wait_send()
    run(xcopy, "wait_send", GRP)
    run(bcopy, "wait_send", NZ)
    run(ccopy, "wait_send", NZ)
    run(ucopy, "wait_send", NZ)
    run(dcopy, "wait_send", GRP)
    run(ocopy, "wait_recv", REP)
    run(ocopy, "wait_send", REP)
    out[...] = orecv[...]


def per_device(tokens, key_weight_base, adapter_down_maps, adapter_up_maps, adapter_index, plan):
    vm = pl.BlockSpec(memory_space=pltpu.VMEM)
    dma = pltpu.SemaphoreType.DMA
    got = pl.pallas_call(
        kernel,
        out_shape=jax.ShapeDtypeStruct((REP, SLOTS, PART), BF16),
        in_specs=[vm] * 6,
        out_specs=vm,
        scratch_shapes=[
            pltpu.VMEM((GRP, PACK // GRP, WIDTH), BF16),
            pltpu.VMEM((GRP, PACK // GRP, WIDTH), BF16),
            pltpu.VMEM((NY, RANK, WIDTH), BF16),
            pltpu.VMEM((NY, RANK, PART), BF16),
            pltpu.VMEM((NZ, ROWS, PART), BF16),
            pltpu.VMEM((NZ, ROWS, PART), BF16),
            pltpu.VMEM((GRP, 32, PART), F32),
            pltpu.VMEM((NZ, 32, PART), F32),
            pltpu.VMEM((32, PART), BF16),
            pltpu.VMEM((NZ, 32, PART), BF16),
            pltpu.VMEM((GRP, PACK // GRP, PART), BF16),
            pltpu.VMEM((GRP, PACK // GRP, PART), BF16),
            pltpu.VMEM((REP, SLOTS, PART), BF16),
            pltpu.VMEM((REP, SLOTS, PART), BF16),
            pltpu.VMEM((ROWS, PART), BF16),
            dma((GRP,)), dma((GRP,)),
            dma((4,)), dma((4,)), dma((3,)), dma((3,)),
            dma((4,)), dma((4,)), dma((3,)), dma((3,)),
            dma((NZ,)), dma((NZ,)),
            dma((NZ,)), dma((NZ,)),
            dma((NZ,)), dma((NZ,)),
            dma((GRP,)), dma((GRP,)),
            dma((REP,)), dma((REP,)),
        ],
        compiler_params=pltpu.CompilerParams(collective_id=0, has_side_effects=True),
        name="keys",
    )(
        tokens, key_weight_base, adapter_down_maps.reshape(WIDTH, RANK),
        adapter_up_maps.reshape(RANK, PART), adapter_index, plan,
    )
    return got.reshape(PACK, PART)


def solution(mesh):
    placed = (
        P("rep", "tp"),
        P("tp", None),
        P("rep", "tp", None),
        P("rep", None, "tp"),
        P("rep", None),
        P("rep", None),
    )
    return jax.shard_map(
        per_device, mesh=mesh, in_specs=placed, out_specs=P("rep", "tp"), check_vma=False
    )
```

```python
import jax
import jax.numpy as jnp
from jax import lax
from jax.experimental import pallas as pl
from jax.experimental.pallas import tpu as pltpu
from jax.sharding import PartitionSpec as P

MESH = pl.DeviceIdType.MESH
F32 = jnp.float32
BF16 = jnp.bfloat16
NX, NY, NC, NZ = 4, 8, 2, 8
REP = NX * NY * NC
GRP = NX * NC
ROWS = 256
WIDTH = 1024
KEYS = 1024
RANK = 64
PART = 128
SLOTS = 8
PACK = REP * SLOTS


def iota(shape, dim):
    return lax.broadcasted_iota(jnp.int32, shape, dim)


def onehot(cond):
    return jnp.where(cond, 1.0, 0.0).astype(BF16)


def kernel(
    tok, w, down, up, ids, dest, out,
    wv, psend, rrecv, maps, bsend, brecv, csend, crecv, usend, urecv, dsend, drecv, osend, orecv,
    s_w, s_x, r_x, s_yr, r_yr, s_yl, r_yl, s_b, r_b, s_c, r_c, s_u, r_u, s_d, r_d, s_o, r_o,
):
    me = lax.axis_index("rep")
    z = lax.axis_index("tp")
    mx = me // (NY * NC)
    my = (me // NC) % NY
    mc = me % NC
    mh = mx * NC + mc

    def rep_of(h, y):
        return ((h // NC) * NY + y) * NC + h % NC

    def grp(k):
        return (mh + k) % GRP

    def zp(k):
        return (z + k) % NZ

    def rep_y(k):
        return rep_of(mh, (my + k) % NY)

    barrier = pltpu.get_barrier_semaphore()
    for k in (1, NY - 1):
        pl.semaphore_signal(barrier, inc=1, device_id={"rep": rep_y(k)}, device_id_type=MESH)
    for k in range(1, GRP):
        pl.semaphore_signal(barrier, inc=1, device_id={"rep": rep_of(grp(k), my)}, device_id_type=MESH)
    for k in range(1, NZ):
        pl.semaphore_signal(barrier, inc=1, device_id={"tp": zp(k)}, device_id_type=MESH)
    load_w = pltpu.make_async_copy(w, wv, s_w)
    load_w.start()

    maps[my, :, :, :WIDTH] = down[...].reshape(2, RANK // 2, WIDTH)
    maps[my, :, :, WIDTH:] = up[...].reshape(2, RANK // 2, PART)

    a = ids[...]
    lane = iota((1, ROWS), 1)
    rank = jnp.zeros((1, ROWS), jnp.int32)
    for k in range(1, SLOTS):
        rank = rank + jnp.where((lane >= k) & (pltpu.roll(a, k, 1) == a), 1, 0)
    ay = (a // NC) % NY
    spot = ((a // (NY * NC)) * NC + a % NC) * (NY * SLOTS) + (ay % 2) * 32 + (ay // 2) * SLOTS + rank
    pick = onehot(iota((PACK, ROWS), 0) == spot)
    for t in range(4):
        cols = slice(256 * t, 256 * t + 256)
        got = jnp.dot(pick, tok[:, cols], preferred_element_type=F32)
        psend[:, :, cols] = got.reshape(GRP, PACK // GRP, 256).astype(BF16)

    pl.semaphore_wait(barrier, 2 + GRP - 1 + NZ - 1)

    def ring(ss, rs, to, step, s, f):
        i = (my + NY + step * s) % NY
        return pltpu.make_async_remote_copy(
            src_ref=maps.at[i, f], dst_ref=maps.at[i, f], send_sem=ss.at[2 * s + f], recv_sem=rs.at[2 * s + f],
            device_id={"rep": to}, device_id_type=MESH)

    hops = [(s, f) for s in range(3) for f in range(2)]
    to_right = {h: ring(s_yr, r_yr, rep_y(1), -1, *h) for h in hops + [(3, 0)]}
    to_left = {h: ring(s_yl, r_yl, rep_y(NY - 1), 1, *h) for h in hops + [(3, 1)]}
    for f in range(2):
        to_right[0, f].start()
        to_left[0, f].start()

    def xcopy(k):
        h = grp(k)
        return pltpu.make_async_remote_copy(
            src_ref=psend.at[h], dst_ref=rrecv.at[mh], send_sem=s_x.at[k], recv_sem=r_x.at[k],
            device_id={"rep": rep_of(h, my)}, device_id_type=MESH)

    def run(make, what, count):
        def body(k, c):
            getattr(make(k), what)()
            return c
        lax.fori_loop(1, count, body, 0)

    run(xcopy, "start", GRP)
    rrecv[mh] = psend[mh]

    load_w.wait()
    for t in range(4):
        got = jnp.dot(tok[...], wv[:, 256 * t:256 * t + 256], preferred_element_type=F32).astype(BF16)
        bsend[2 * t] = got[:, :PART]
        bsend[2 * t + 1] = got[:, PART:]

    def zcopy(src, dst, ss, rs):
        def make(k):
            return pltpu.make_async_remote_copy(
                src_ref=src(zp(k)), dst_ref=dst.at[z], send_sem=ss.at[k], recv_sem=rs.at[k],
                device_id={"tp": zp(k)}, device_id_type=MESH)
        return make

    bcopy = zcopy(lambda t: bsend.at[t], brecv, s_b, r_b)
    run(bcopy, "start", NZ)
    brecv[z] = bsend[z]

    square = iota((ROWS, ROWS), 0) == iota((ROWS, ROWS), 1)
    spot_col = jnp.sum(jnp.where(square, spot.astype(F32), 0.0), axis=1, keepdims=True).astype(jnp.int32)
    back = onehot(iota((ROWS, PACK), 1) == spot_col)
    d_row = dest[...]
    d_col = jnp.sum(jnp.where(square, d_row.astype(F32), 0.0), axis=1, keepdims=True).astype(jnp.int32)
    earlier = (d_col == d_row) & (iota((ROWS, ROWS), 0) < iota((ROWS, ROWS), 1))
    slot = jnp.sum(jnp.where(earlier, 1.0, 0.0), axis=0, keepdims=True).astype(jnp.int32)
    place = onehot(iota((PACK, ROWS), 0) == d_row * SLOTS + slot)

    for s, f in hops:
        for way in (to_right, to_left):
            way[s, f].wait_recv()
            if (s + 1, f) in way:
                way[s + 1, f].start()
    to_right[3, 0].wait_recv()
    to_left[3, 1].wait_recv()
    run(xcopy, "wait_recv", GRP)

    r_all = rrecv[...].reshape(PACK, WIDTH)
    fold = jnp.zeros((PACK, PART), F32)
    row = iota((PACK, PART), 0)
    half = iota((PACK, PART), 1) // RANK
    mine = (row % 64) // 32 == half
    for t in range(2):
        d4 = maps[4 * t:4 * t + 4, :, :, :WIDTH].reshape(4 * RANK, WIDTH)
        got = lax.dot_general(r_all, d4, (((1,), (1,)), ((), ())), preferred_element_type=F32)
        for i in range(2):
            keep = mine & ((row % 32) // SLOTS == 2 * t + i)
            fold = fold + jnp.where(keep, got[:, PART * i:PART * i + PART], 0.0)
    fold = fold.reshape(GRP, 2, 32, PART)
    csend[...] = (fold[:, 0] + fold[:, 1]).astype(BF16)
    ccopy = zcopy(lambda t: csend.at[t], crecv, s_c, r_c)
    run(ccopy, "start", NZ)
    crecv[z] = csend[z]
    run(bcopy, "wait_recv", NZ)
    base = jnp.sum(brecv[...].astype(F32), axis=0)
    run(ccopy, "wait_recv", NZ)
    usend[...] = jnp.sum(crecv[...].astype(F32), axis=0).astype(BF16)
    ucopy = zcopy(lambda t: usend, urecv, s_u, r_u)
    run(ucopy, "start", NZ)
    urecv[z] = usend[...]
    run(ucopy, "wait_recv", NZ)

    u = urecv[...].astype(F32).reshape(NZ, 4, SLOTS, PART)
    first = iota((NZ * SLOTS, PART), 1) < RANK
    for i in range(4):
        ui = u[:, i].reshape(NZ * SLOTS, PART)
        both = jnp.concatenate([jnp.where(first, ui, 0.0), jnp.where(first, 0.0, ui)], axis=0).astype(BF16)
        up2 = maps[2 * i:2 * i + 2, :, :, WIDTH:].reshape(2 * RANK, PART)
        got = jnp.dot(both, up2, preferred_element_type=F32).astype(BF16)
        got = got.reshape(2, NZ, SLOTS, PART)
        for p in range(2):
            dsend[:, 32 * p + SLOTS * i:32 * p + SLOTS * i + SLOTS] = got[p]

    def dcopy(k):
        h = grp(k)
        return pltpu.make_async_remote_copy(
            src_ref=dsend.at[h], dst_ref=drecv.at[mh], send_sem=s_d.at[k], recv_sem=r_d.at[k],
            device_id={"rep": rep_of(h, my)}, device_id_type=MESH)

    run(dcopy, "start", GRP)
    drecv[mh] = dsend[mh]
    run(dcopy, "wait_recv", GRP)

    delta = jnp.dot(back, drecv[...].reshape(PACK, PART), preferred_element_type=F32)
    keyrow = (base + 2.0 * delta).astype(BF16)
    got = jnp.dot(place, keyrow, preferred_element_type=F32)
    osend[...] = got.reshape(REP, SLOTS, PART).astype(BF16)

    def ocopy(k):
        to = (me + k) % REP
        return pltpu.make_async_remote_copy(
            src_ref=osend.at[to], dst_ref=orecv.at[me], send_sem=s_o.at[k], recv_sem=r_o.at[k],
            device_id={"rep": to}, device_id_type=MESH)

    run(ocopy, "start", REP)
    orecv[me] = osend[me]
    for way in (to_right, to_left):
        for c in way.values():
            c.wait_send()
    run(xcopy, "wait_send", GRP)
    run(bcopy, "wait_send", NZ)
    run(ccopy, "wait_send", NZ)
    run(ucopy, "wait_send", NZ)
    run(dcopy, "wait_send", GRP)
    run(ocopy, "wait_recv", REP)
    run(ocopy, "wait_send", REP)
    out[...] = orecv[...]


def per_device(tokens, key_weight_base, adapter_down_maps, adapter_up_maps, adapter_index, plan):
    vm = pl.BlockSpec(memory_space=pltpu.VMEM)
    dma = pltpu.SemaphoreType.DMA
    got = pl.pallas_call(
        kernel,
        out_shape=jax.ShapeDtypeStruct((REP, SLOTS, PART), BF16),
        in_specs=[vm, pl.BlockSpec(memory_space=pl.ANY)] + [vm] * 4,
        out_specs=vm,
        scratch_shapes=[
            pltpu.VMEM((WIDTH, KEYS), BF16),
            pltpu.VMEM((GRP, PACK // GRP, WIDTH), BF16),
            pltpu.VMEM((GRP, PACK // GRP, WIDTH), BF16),
            pltpu.VMEM((NY, 2, RANK // 2, WIDTH + PART), BF16),
            pltpu.VMEM((NZ, ROWS, PART), BF16),
            pltpu.VMEM((NZ, ROWS, PART), BF16),
            pltpu.VMEM((GRP, 32, PART), BF16),
            pltpu.VMEM((NZ, 32, PART), BF16),
            pltpu.VMEM((32, PART), BF16),
            pltpu.VMEM((NZ, 32, PART), BF16),
            pltpu.VMEM((GRP, PACK // GRP, PART), BF16),
            pltpu.VMEM((GRP, PACK // GRP, PART), BF16),
            pltpu.VMEM((REP, SLOTS, PART), BF16),
            pltpu.VMEM((REP, SLOTS, PART), BF16),
            dma(()), dma((GRP,)), dma((GRP,)),
            dma((8,)), dma((8,)), dma((8,)), dma((8,)),
            dma((NZ,)), dma((NZ,)),
            dma((NZ,)), dma((NZ,)),
            dma((NZ,)), dma((NZ,)),
            dma((GRP,)), dma((GRP,)),
            dma((REP,)), dma((REP,)),
        ],
        compiler_params=pltpu.CompilerParams(collective_id=0, has_side_effects=True),
        name="keys",
    )(
        tokens, key_weight_base, adapter_down_maps.reshape(WIDTH, RANK).T,
        adapter_up_maps.reshape(RANK, PART), adapter_index, plan.reshape(1, ROWS),
    )
    return got.reshape(PACK, PART)


def solution(mesh):
    placed = (
        P("rep", "tp"),
        P("tp", None),
        P("rep", "tp", None),
        P("rep", None, "tp"),
        P("rep", None),
        P("rep", None),
    )
    return jax.shard_map(
        per_device, mesh=mesh, in_specs=placed, out_specs=P("rep", "tp"), check_vma=False
    )
```

```python
import jax
import jax.numpy as jnp
from jax import lax
from jax.experimental import pallas as pl
from jax.experimental.pallas import tpu as pltpu
from jax.sharding import PartitionSpec as P

MESH = pl.DeviceIdType.MESH
F32 = jnp.float32
BF16 = jnp.bfloat16
NX, NY, NC, NZ = 4, 8, 2, 8
REP = NX * NY * NC
GRP = NX * NC
ROWS = 256
WIDTH = 1024
KEYS = 1024
RANK = 64
PART = 128
SLOTS = 8
PACK = REP * SLOTS
PIECES = 4


def iota(shape, dim):
    return lax.broadcasted_iota(jnp.int32, shape, dim)


def onehot(cond):
    return jnp.where(cond, 1.0, 0.0).astype(BF16)


def kernel(
    tok, w, down, up, ids, dest, out,
    wv, psend, rrecv, maps, bsend, brecv, csend, crecv, usend, urecv, dsend, drecv, osend, orecv,
    s_w, s_x, r_x, s_yr, r_yr, s_yl, r_yl, s_b, r_b, s_c, r_c, s_u, r_u, s_d, r_d, s_o, r_o,
):
    me = lax.axis_index("rep")
    z = lax.axis_index("tp")
    mx = me // (NY * NC)
    my = (me // NC) % NY
    mc = me % NC
    mh = mx * NC + mc

    def rep_of(h, y):
        return ((h // NC) * NY + y) * NC + h % NC

    def far(n, ring):
        return ring // 2 + (1 - 2 * (n % 2)) * ((n + 1) // 2)

    def grp(n):
        return ((mx + far(n // NC, NX)) % NX) * NC + (mc + 1 - n % NC) % NC

    def zp(n):
        return (z + far(n, NZ)) % NZ

    def anyone(n):
        return rep_of(grp(n % GRP), (my + far(n // GRP, NY)) % NY)

    def rep_y(k):
        return rep_of(mh, (my + k) % NY)

    barrier = pltpu.get_barrier_semaphore()
    for k in (1, NY - 1):
        pl.semaphore_signal(barrier, inc=1, device_id={"rep": rep_y(k)}, device_id_type=MESH)
    for k in range(GRP - 1):
        pl.semaphore_signal(barrier, inc=1, device_id={"rep": rep_of(grp(k), my)}, device_id_type=MESH)
    for k in range(NZ - 1):
        pl.semaphore_signal(barrier, inc=1, device_id={"tp": zp(k)}, device_id_type=MESH)
    load_w = pltpu.make_async_copy(w, wv, s_w)
    load_w.start()

    maps[my, :, :, :WIDTH] = down[...].reshape(PIECES, RANK // PIECES, WIDTH)
    maps[my, :, :, WIDTH:] = up[...].reshape(PIECES, RANK // PIECES, PART)

    a = ids[...]
    lane = iota((1, ROWS), 1)
    rank = jnp.zeros((1, ROWS), jnp.int32)
    for k in range(1, SLOTS):
        rank = rank + jnp.where((lane >= k) & (pltpu.roll(a, k, 1) == a), 1, 0)
    ay = (a // NC) % NY
    spot = ((a // (NY * NC)) * NC + a % NC) * (NY * SLOTS) + (ay % 2) * 32 + (ay // 2) * SLOTS + rank
    pick = onehot(iota((PACK, ROWS), 0) == spot)
    for t in range(4):
        cols = slice(256 * t, 256 * t + 256)
        got = jnp.dot(pick, tok[:, cols], preferred_element_type=F32)
        psend[:, :, cols] = got.reshape(GRP, PACK // GRP, 256).astype(BF16)

    pl.semaphore_wait(barrier, 2 + GRP - 1 + NZ - 1)

    def ring(ss, rs, to, step, s, f):
        i = (my + NY + step * s) % NY
        return pltpu.make_async_remote_copy(
            src_ref=maps.at[i, f], dst_ref=maps.at[i, f], send_sem=ss.at[PIECES * s + f], recv_sem=rs.at[PIECES * s + f],
            device_id={"rep": to}, device_id_type=MESH)

    hops = [(s, f) for s in range(3) for f in range(PIECES)]
    last_right = [(3, f) for f in range(PIECES // 2)]
    last_left = [(3, f) for f in range(PIECES // 2, PIECES)]
    to_right = {h: ring(s_yr, r_yr, rep_y(1), -1, *h) for h in hops + last_right}
    to_left = {h: ring(s_yl, r_yl, rep_y(NY - 1), 1, *h) for h in hops + last_left}
    for f in range(PIECES):
        to_right[0, f].start()
        to_left[0, f].start()

    def xcopy(k):
        h = grp(k)
        return pltpu.make_async_remote_copy(
            src_ref=psend.at[h], dst_ref=rrecv.at[mh], send_sem=s_x.at[k], recv_sem=r_x.at[k],
            device_id={"rep": rep_of(h, my)}, device_id_type=MESH)

    def run(make, what, count):
        def body(k, c):
            getattr(make(k), what)()
            return c
        lax.fori_loop(0, count - 1, body, 0)

    run(xcopy, "start", GRP)
    rrecv[mh] = psend[mh]

    load_w.wait()
    for t in range(4):
        got = jnp.dot(tok[...], wv[:, 256 * t:256 * t + 256], preferred_element_type=F32).astype(BF16)
        bsend[2 * t] = got[:, :PART]
        bsend[2 * t + 1] = got[:, PART:]

    def zcopy(src, dst, ss, rs):
        def make(k):
            return pltpu.make_async_remote_copy(
                src_ref=src(zp(k)), dst_ref=dst.at[z], send_sem=ss.at[k], recv_sem=rs.at[k],
                device_id={"tp": zp(k)}, device_id_type=MESH)
        return make

    bcopy = zcopy(lambda t: bsend.at[t], brecv, s_b, r_b)
    run(bcopy, "start", NZ)
    brecv[z] = bsend[z]

    square = iota((ROWS, ROWS), 0) == iota((ROWS, ROWS), 1)
    spot_col = jnp.sum(jnp.where(square, spot.astype(F32), 0.0), axis=1, keepdims=True).astype(jnp.int32)
    back = onehot(iota((ROWS, PACK), 1) == spot_col)
    d_row = dest[...]
    d_col = jnp.sum(jnp.where(square, d_row.astype(F32), 0.0), axis=1, keepdims=True).astype(jnp.int32)
    earlier = (d_col == d_row) & (iota((ROWS, ROWS), 0) < iota((ROWS, ROWS), 1))
    slot = jnp.sum(jnp.where(earlier, 1.0, 0.0), axis=0, keepdims=True).astype(jnp.int32)
    place = onehot(iota((PACK, ROWS), 0) == d_row * SLOTS + slot)

    for s, f in hops:
        for way in (to_right, to_left):
            way[s, f].wait_recv()
            if (s + 1, f) in way:
                way[s + 1, f].start()
    for h in last_right:
        to_right[h].wait_recv()
    for h in last_left:
        to_left[h].wait_recv()
    run(xcopy, "wait_recv", GRP)

    r_all = rrecv[...].reshape(PACK, WIDTH)
    fold = jnp.zeros((PACK, PART), F32)
    row = iota((PACK, PART), 0)
    half = iota((PACK, PART), 1) // RANK
    mine = (row % 64) // 32 == half
    for t in range(2):
        d4 = maps[4 * t:4 * t + 4, :, :, :WIDTH].reshape(4 * RANK, WIDTH)
        got = lax.dot_general(r_all, d4, (((1,), (1,)), ((), ())), preferred_element_type=F32)
        for i in range(2):
            keep = mine & ((row % 32) // SLOTS == 2 * t + i)
            fold = fold + jnp.where(keep, got[:, PART * i:PART * i + PART], 0.0)
    fold = fold.reshape(GRP, 2, 32, PART)
    csend[...] = fold[:, 0] + fold[:, 1]
    ccopy = zcopy(lambda t: csend.at[t], crecv, s_c, r_c)
    run(ccopy, "start", NZ)
    crecv[z] = csend[z]
    run(bcopy, "wait_recv", NZ)
    base = jnp.sum(brecv[...].astype(F32), axis=0)
    run(ccopy, "wait_recv", NZ)
    usend[...] = jnp.sum(crecv[...], axis=0).astype(BF16)
    ucopy = zcopy(lambda t: usend, urecv, s_u, r_u)
    run(ucopy, "start", NZ)
    urecv[z] = usend[...]
    run(ucopy, "wait_recv", NZ)

    u = urecv[...].astype(F32).reshape(NZ, 4, SLOTS, PART)
    first = iota((NZ * SLOTS, PART), 1) < RANK
    for i in range(4):
        ui = u[:, i].reshape(NZ * SLOTS, PART)
        both = jnp.concatenate([jnp.where(first, ui, 0.0), jnp.where(first, 0.0, ui)], axis=0).astype(BF16)
        up2 = maps[2 * i:2 * i + 2, :, :, WIDTH:].reshape(2 * RANK, PART)
        got = jnp.dot(both, up2, preferred_element_type=F32).astype(BF16)
        got = got.reshape(2, NZ, SLOTS, PART)
        for p in range(2):
            dsend[:, 32 * p + SLOTS * i:32 * p + SLOTS * i + SLOTS] = got[p]

    def dcopy(k):
        h = grp(k)
        return pltpu.make_async_remote_copy(
            src_ref=dsend.at[h], dst_ref=drecv.at[mh], send_sem=s_d.at[k], recv_sem=r_d.at[k],
            device_id={"rep": rep_of(h, my)}, device_id_type=MESH)

    run(dcopy, "start", GRP)
    drecv[mh] = dsend[mh]
    run(dcopy, "wait_recv", GRP)

    delta = jnp.dot(back, drecv[...].reshape(PACK, PART), preferred_element_type=F32)
    keyrow = (base + 2.0 * delta).astype(BF16)
    got = jnp.dot(place, keyrow, preferred_element_type=F32)
    osend[...] = got.reshape(REP, SLOTS, PART).astype(BF16)

    def ocopy(k):
        to = anyone(k)
        return pltpu.make_async_remote_copy(
            src_ref=osend.at[to], dst_ref=orecv.at[me], send_sem=s_o.at[k], recv_sem=r_o.at[k],
            device_id={"rep": to}, device_id_type=MESH)

    run(ocopy, "start", REP)
    orecv[me] = osend[me]
    for way in (to_right, to_left):
        for c in way.values():
            c.wait_send()
    run(xcopy, "wait_send", GRP)
    run(bcopy, "wait_send", NZ)
    run(ccopy, "wait_send", NZ)
    run(ucopy, "wait_send", NZ)
    run(dcopy, "wait_send", GRP)
    run(ocopy, "wait_recv", REP)
    run(ocopy, "wait_send", REP)
    out[...] = orecv[...]


def per_device(tokens, key_weight_base, adapter_down_maps, adapter_up_maps, adapter_index, plan):
    vm = pl.BlockSpec(memory_space=pltpu.VMEM)
    dma = pltpu.SemaphoreType.DMA
    got = pl.pallas_call(
        kernel,
        out_shape=jax.ShapeDtypeStruct((REP, SLOTS, PART), BF16),
        in_specs=[vm, pl.BlockSpec(memory_space=pl.ANY)] + [vm] * 4,
        out_specs=vm,
        scratch_shapes=[
            pltpu.VMEM((WIDTH, KEYS), BF16),
            pltpu.VMEM((GRP, PACK // GRP, WIDTH), BF16),
            pltpu.VMEM((GRP, PACK // GRP, WIDTH), BF16),
            pltpu.VMEM((NY, PIECES, RANK // PIECES, WIDTH + PART), BF16),
            pltpu.VMEM((NZ, ROWS, PART), BF16),
            pltpu.VMEM((NZ, ROWS, PART), BF16),
            pltpu.VMEM((GRP, 32, PART), F32),
            pltpu.VMEM((NZ, 32, PART), F32),
            pltpu.VMEM((32, PART), BF16),
            pltpu.VMEM((NZ, 32, PART), BF16),
            pltpu.VMEM((GRP, PACK // GRP, PART), BF16),
            pltpu.VMEM((GRP, PACK // GRP, PART), BF16),
            pltpu.VMEM((REP, SLOTS, PART), BF16),
            pltpu.VMEM((REP, SLOTS, PART), BF16),
            dma(()), dma((GRP,)), dma((GRP,)),
            dma((4 * PIECES,)), dma((4 * PIECES,)), dma((4 * PIECES,)), dma((4 * PIECES,)),
            dma((NZ,)), dma((NZ,)),
            dma((NZ,)), dma((NZ,)),
            dma((NZ,)), dma((NZ,)),
            dma((GRP,)), dma((GRP,)),
            dma((REP,)), dma((REP,)),
        ],
        compiler_params=pltpu.CompilerParams(collective_id=0, has_side_effects=True),
        name="keys",
    )(
        tokens, key_weight_base, adapter_down_maps.reshape(WIDTH, RANK).T,
        adapter_up_maps.reshape(RANK, PART), adapter_index, plan.reshape(1, ROWS),
    )
    return got.reshape(PACK, PART)


def solution(mesh):
    placed = (
        P("rep", "tp"),
        P("tp", None),
        P("rep", "tp", None),
        P("rep", None, "tp"),
        P("rep", None),
        P("rep", None),
    )
    return jax.shard_map(
        per_device, mesh=mesh, in_specs=placed, out_specs=P("rep", "tp"), check_vma=False
    )
```

```python
import jax
import jax.numpy as jnp
from jax import lax
from jax.experimental import pallas as pl
from jax.experimental.pallas import tpu as pltpu
from jax.sharding import PartitionSpec as P

MESH = pl.DeviceIdType.MESH
F32 = jnp.float32
BF16 = jnp.bfloat16
NX, NY, NC, NZ = 4, 8, 2, 8
REP = NX * NY * NC
GRP = NX * NC
ROWS = 256
WIDTH = 1024
KEYS = 1024
RANK = 64
PART = 128
SLOTS = 8
PACK = REP * SLOTS
PIECES = 4


def iota(shape, dim):
    return lax.broadcasted_iota(jnp.int32, shape, dim)


def onehot(cond):
    return jnp.where(cond, 1.0, 0.0).astype(BF16)


def kernel(
    tok_in, w_in, down_in, up_in, ids_in, dest_in, out,
    tok, w, ids, dest, psend, rrecv, maps, ups, bsend, brecv, csend, crecv, usend, urecv, dsend, drecv, osend, orecv,
    s_in, s_m, r_m, s_x, r_x, s_yr, r_yr, s_yl, r_yl, s_b, r_b, s_c, r_c, s_u, r_u, s_d, r_d, s_o, r_o,
):
    me = lax.axis_index("rep")
    z = lax.axis_index("tp")
    mx = me // (NY * NC)
    my = (me // NC) % NY
    mc = me % NC
    mh = mx * NC + mc

    def rep_of(h, y):
        return ((h // NC) * NY + y) * NC + h % NC

    def far(n, ring):
        return ring // 2 + (1 - 2 * (n % 2)) * ((n + 1) // 2)

    def grp(n):
        return ((mx + far(n // NC, NX)) % NX) * NC + (mc + 1 - n % NC) % NC

    def zp(n):
        return (z + far(n, NZ)) % NZ

    def anyone(n):
        return rep_of(grp(n % GRP), (my + far(n // GRP, NY)) % NY)

    def rep_y(k):
        return rep_of(mh, (my + k) % NY)

    barrier = pltpu.get_barrier_semaphore()
    for k in (1, NY - 1):
        pl.semaphore_signal(barrier, inc=1, device_id={"rep": rep_y(k)}, device_id_type=MESH)
    for k in range(GRP - 1):
        pl.semaphore_signal(barrier, inc=1, device_id={"rep": rep_of(grp(k), my)}, device_id_type=MESH)
    for k in range(NZ - 1):
        pl.semaphore_signal(barrier, inc=1, device_id={"tp": zp(k)}, device_id_type=MESH)

    loads = [
        pltpu.make_async_copy(src, dst, s_in.at[n]) for n, (src, dst) in enumerate((
            (ids_in, ids), (dest_in, dest), (down_in, maps.at[my]), (tok_in, tok), (w_in, w), (up_in, ups.at[my])))
    ]
    for c in loads:
        c.start()
    loads[0].wait()

    a = ids[...]
    lane = iota((1, ROWS), 1)
    rank = jnp.zeros((1, ROWS), jnp.int32)
    for k in range(1, SLOTS):
        rank = rank + jnp.where((lane >= k) & (pltpu.roll(a, k, 1) == a), 1, 0)
    ay = (a // NC) % NY
    spot = ((a // (NY * NC)) * NC + a % NC) * (NY * SLOTS) + (ay % 2) * 32 + (ay // 2) * SLOTS + rank
    pick = onehot(iota((PACK, ROWS), 0) == spot)
    loads[3].wait()
    for t in range(4):
        cols = slice(256 * t, 256 * t + 256)
        got = jnp.dot(pick, tok[:, cols], preferred_element_type=F32)
        psend[:, :, cols] = got.reshape(GRP, PACK // GRP, 256).astype(BF16)

    loads[2].wait()
    pl.semaphore_wait(barrier, 2 + GRP - 1 + NZ - 1)

    def ring(ss, rs, to, step, s, f):
        i = (my + NY + step * s) % NY
        return pltpu.make_async_remote_copy(
            src_ref=maps.at[i, f], dst_ref=maps.at[i, f], send_sem=ss.at[PIECES * s + f], recv_sem=rs.at[PIECES * s + f],
            device_id={"rep": to}, device_id_type=MESH)

    hops = [(s, f) for s in range(3) for f in range(PIECES)]
    last_right = [(3, f) for f in range(PIECES // 2)]
    last_left = [(3, f) for f in range(PIECES // 2, PIECES)]
    to_right = {h: ring(s_yr, r_yr, rep_y(1), -1, *h) for h in hops + last_right}
    to_left = {h: ring(s_yl, r_yl, rep_y(NY - 1), 1, *h) for h in hops + last_left}
    for f in range(PIECES):
        to_right[0, f].start()
        to_left[0, f].start()

    def xcopy(k):
        h = grp(k)
        return pltpu.make_async_remote_copy(
            src_ref=psend.at[h], dst_ref=rrecv.at[mh], send_sem=s_x.at[k], recv_sem=r_x.at[k],
            device_id={"rep": rep_of(h, my)}, device_id_type=MESH)

    def run(make, what, count):
        def body(k, c):
            getattr(make(k), what)()
            return c
        lax.fori_loop(0, count - 1, body, 0)

    run(xcopy, "start", GRP)
    rrecv[mh] = psend[mh]

    loads[4].wait()
    for t in range(4):
        got = jnp.dot(tok[...], w[:, 256 * t:256 * t + 256], preferred_element_type=F32).astype(BF16)
        bsend[2 * t] = got[:, :PART]
        bsend[2 * t + 1] = got[:, PART:]

    def zcopy(src, dst, ss, rs):
        def make(k):
            return pltpu.make_async_remote_copy(
                src_ref=src(zp(k)), dst_ref=dst.at[z], send_sem=ss.at[k], recv_sem=rs.at[k],
                device_id={"tp": zp(k)}, device_id_type=MESH)
        return make

    bcopy = zcopy(lambda t: bsend.at[t], brecv, s_b, r_b)
    run(bcopy, "start", NZ)
    brecv[z] = bsend[z]

    square = iota((ROWS, ROWS), 0) == iota((ROWS, ROWS), 1)
    spot_col = jnp.sum(jnp.where(square, spot.astype(F32), 0.0), axis=1, keepdims=True).astype(jnp.int32)
    back = onehot(iota((ROWS, PACK), 1) == spot_col)
    loads[1].wait()
    loads[5].wait()
    d_row = dest[...]
    d_col = jnp.sum(jnp.where(square, d_row.astype(F32), 0.0), axis=1, keepdims=True).astype(jnp.int32)
    earlier = (d_col == d_row) & (iota((ROWS, ROWS), 0) < iota((ROWS, ROWS), 1))
    slot = jnp.sum(jnp.where(earlier, 1.0, 0.0), axis=0, keepdims=True).astype(jnp.int32)
    place = onehot(iota((PACK, ROWS), 0) == d_row * SLOTS + slot)

    for s, f in hops:
        for way in (to_right, to_left):
            way[s, f].wait_recv()
            if (s + 1, f) in way:
                way[s + 1, f].start()
    for h in last_right:
        to_right[h].wait_recv()
    for h in last_left:
        to_left[h].wait_recv()

    def mcopy(k):
        return pltpu.make_async_remote_copy(
            src_ref=ups.at[my], dst_ref=ups.at[my], send_sem=s_m.at[k], recv_sem=r_m.at[k],
            device_id={"rep": rep_y(far(k, NY))}, device_id_type=MESH)

    run(mcopy, "start", NY)
    run(xcopy, "wait_recv", GRP)

    r_all = rrecv[...].reshape(PACK, WIDTH)
    fold = jnp.zeros((PACK, PART), F32)
    row = iota((PACK, PART), 0)
    half = iota((PACK, PART), 1) // RANK
    mine = (row % 64) // 32 == half
    for t in range(2):
        d4 = maps[4 * t:4 * t + 4].reshape(4 * RANK, WIDTH)
        got = lax.dot_general(r_all, d4, (((1,), (1,)), ((), ())), preferred_element_type=F32)
        for i in range(2):
            keep = mine & ((row % 32) // SLOTS == 2 * t + i)
            fold = fold + jnp.where(keep, got[:, PART * i:PART * i + PART], 0.0)
    fold = fold.reshape(GRP, 2, 32, PART)
    csend[...] = fold[:, 0] + fold[:, 1]
    ccopy = zcopy(lambda t: csend.at[t], crecv, s_c, r_c)
    run(ccopy, "start", NZ)
    crecv[z] = csend[z]
    run(bcopy, "wait_recv", NZ)
    base = jnp.sum(brecv[...].astype(F32), axis=0)
    run(ccopy, "wait_recv", NZ)
    usend[...] = jnp.sum(crecv[...], axis=0).astype(BF16)
    ucopy = zcopy(lambda t: usend, urecv, s_u, r_u)
    run(ucopy, "start", NZ)
    urecv[z] = usend[...]
    run(ucopy, "wait_recv", NZ)

    run(mcopy, "wait_recv", NY)
    u = urecv[...].astype(F32).reshape(NZ, 4, SLOTS, PART)
    first = iota((NZ * SLOTS, PART), 1) < RANK
    for i in range(4):
        ui = u[:, i].reshape(NZ * SLOTS, PART)
        both = jnp.concatenate([jnp.where(first, ui, 0.0), jnp.where(first, 0.0, ui)], axis=0).astype(BF16)
        up2 = ups[2 * i:2 * i + 2].reshape(2 * RANK, PART)
        got = jnp.dot(both, up2, preferred_element_type=F32).astype(BF16)
        got = got.reshape(2, NZ, SLOTS, PART)
        for p in range(2):
            dsend[:, 32 * p + SLOTS * i:32 * p + SLOTS * i + SLOTS] = got[p]

    def dcopy(k):
        h = grp(k)
        return pltpu.make_async_remote_copy(
            src_ref=dsend.at[h], dst_ref=drecv.at[mh], send_sem=s_d.at[k], recv_sem=r_d.at[k],
            device_id={"rep": rep_of(h, my)}, device_id_type=MESH)

    run(dcopy, "start", GRP)
    drecv[mh] = dsend[mh]
    run(dcopy, "wait_recv", GRP)

    delta = jnp.dot(back, drecv[...].reshape(PACK, PART), preferred_element_type=F32)
    keyrow = (base + 2.0 * delta).astype(BF16)
    got = jnp.dot(place, keyrow, preferred_element_type=F32)
    osend[...] = got.reshape(REP, SLOTS, PART).astype(BF16)

    def ocopy(k):
        to = anyone(k)
        return pltpu.make_async_remote_copy(
            src_ref=osend.at[to], dst_ref=orecv.at[me], send_sem=s_o.at[k], recv_sem=r_o.at[k],
            device_id={"rep": to}, device_id_type=MESH)

    run(ocopy, "start", REP)
    orecv[me] = osend[me]
    for way in (to_right, to_left):
        for c in way.values():
            c.wait_send()
    run(mcopy, "wait_send", NY)
    run(xcopy, "wait_send", GRP)
    run(bcopy, "wait_send", NZ)
    run(ccopy, "wait_send", NZ)
    run(ucopy, "wait_send", NZ)
    run(dcopy, "wait_send", GRP)
    run(ocopy, "wait_recv", REP)
    run(ocopy, "wait_send", REP)
    out[...] = orecv[...]


def per_device(tokens, key_weight_base, adapter_down_maps, adapter_up_maps, adapter_index, plan):
    vm = pl.BlockSpec(memory_space=pltpu.VMEM)
    dma = pltpu.SemaphoreType.DMA
    got = pl.pallas_call(
        kernel,
        out_shape=jax.ShapeDtypeStruct((REP, SLOTS, PART), BF16),
        in_specs=[pl.BlockSpec(memory_space=pl.ANY)] * 6,
        out_specs=vm,
        scratch_shapes=[
            pltpu.VMEM((ROWS, WIDTH), BF16),
            pltpu.VMEM((WIDTH, KEYS), BF16),
            pltpu.VMEM((1, ROWS), jnp.int32),
            pltpu.VMEM((1, ROWS), jnp.int32),
            pltpu.VMEM((GRP, PACK // GRP, WIDTH), BF16),
            pltpu.VMEM((GRP, PACK // GRP, WIDTH), BF16),
            pltpu.VMEM((NY, PIECES, RANK // PIECES, WIDTH), BF16),
            pltpu.VMEM((NY, RANK, PART), BF16),
            pltpu.VMEM((NZ, ROWS, PART), BF16),
            pltpu.VMEM((NZ, ROWS, PART), BF16),
            pltpu.VMEM((GRP, 32, PART), F32),
            pltpu.VMEM((NZ, 32, PART), F32),
            pltpu.VMEM((32, PART), BF16),
            pltpu.VMEM((NZ, 32, PART), BF16),
            pltpu.VMEM((GRP, PACK // GRP, PART), BF16),
            pltpu.VMEM((GRP, PACK // GRP, PART), BF16),
            pltpu.VMEM((REP, SLOTS, PART), BF16),
            pltpu.VMEM((REP, SLOTS, PART), BF16),
            dma((6,)), dma((NY,)), dma((NY,)), dma((GRP,)), dma((GRP,)),
            dma((4 * PIECES,)), dma((4 * PIECES,)), dma((4 * PIECES,)), dma((4 * PIECES,)),
            dma((NZ,)), dma((NZ,)),
            dma((NZ,)), dma((NZ,)),
            dma((NZ,)), dma((NZ,)),
            dma((GRP,)), dma((GRP,)),
            dma((REP,)), dma((REP,)),
        ],
        compiler_params=pltpu.CompilerParams(collective_id=0, has_side_effects=True),
        name="keys",
    )(
        tokens, key_weight_base, adapter_down_maps.reshape(WIDTH, RANK).T.reshape(PIECES, RANK // PIECES, WIDTH),
        adapter_up_maps.reshape(RANK, PART), adapter_index, plan.reshape(1, ROWS),
    )
    return got.reshape(PACK, PART)


def solution(mesh):
    placed = (
        P("rep", "tp"),
        P("tp", None),
        P("rep", "tp", None),
        P("rep", None, "tp"),
        P("rep", None),
        P("rep", None),
    )
    return jax.shard_map(
        per_device, mesh=mesh, in_specs=placed, out_specs=P("rep", "tp"), check_vma=False
    )
```

```python
import jax
import jax.numpy as jnp
from jax import lax
from jax.experimental import pallas as pl
from jax.experimental.pallas import tpu as pltpu
from jax.sharding import PartitionSpec as P

MESH = pl.DeviceIdType.MESH
F32 = jnp.float32
BF16 = jnp.bfloat16
NX, NY, NC, NZ = 4, 8, 2, 8
REP = NX * NY * NC
GRP = NX * NC
ROWS = 256
WIDTH = 1024
KEYS = 1024
RANK = 64
PART = 128
SLOTS = 8
PACK = REP * SLOTS
PIECES = 4


def iota(shape, dim):
    return lax.broadcasted_iota(jnp.int32, shape, dim)


def onehot(cond):
    return jnp.where(cond, 1.0, 0.0).astype(BF16)


def kernel(
    tok_in, w_in, down_in, up_in, ids_in, dest_in, out,
    tok, w, ids, dest, psend, rrecv, maps, ups, bsend, brecv, csend, crecv, usend, urecv, dsend, drecv, osend, orecv,
    s_in, s_m, r_m, s_x, r_x, s_yr, r_yr, s_yl, r_yl, s_b, r_b, s_c, r_c, s_u, r_u, s_d, r_d, s_o, r_o,
):
    me = lax.axis_index("rep")
    z = lax.axis_index("tp")
    mx = me // (NY * NC)
    my = (me // NC) % NY
    mc = me % NC
    mh = mx * NC + mc

    def rep_of(h, y):
        return ((h // NC) * NY + y) * NC + h % NC

    def far(n, ring):
        return ring // 2 + (1 - 2 * (n % 2)) * ((n + 1) // 2)

    def grp(n):
        return ((mx + far(n // NC, NX)) % NX) * NC + (mc + 1 - n % NC) % NC

    def zp(n):
        return (z + far(n, NZ)) % NZ

    def anyone(n):
        return rep_of(grp(n % GRP), (my + far(n // GRP, NY)) % NY)

    def rep_y(k):
        return rep_of(mh, (my + k) % NY)

    barrier = pltpu.get_barrier_semaphore()
    for k in (1, NY - 1):
        pl.semaphore_signal(barrier, inc=1, device_id={"rep": rep_y(k)}, device_id_type=MESH)
    for k in range(GRP - 1):
        pl.semaphore_signal(barrier, inc=1, device_id={"rep": rep_of(grp(k), my)}, device_id_type=MESH)
    for k in range(NZ - 1):
        pl.semaphore_signal(barrier, inc=1, device_id={"tp": zp(k)}, device_id_type=MESH)

    loads = [
        pltpu.make_async_copy(src, dst, s_in.at[n]) for n, (src, dst) in enumerate((
            (ids_in, ids), (dest_in, dest), (down_in, maps.at[my]), (tok_in, tok), (w_in, w), (up_in, ups.at[my])))
    ]
    for c in loads:
        c.start()
    loads[0].wait()

    a = ids[...]
    lane = iota((1, ROWS), 1)
    rank = jnp.zeros((1, ROWS), jnp.int32)
    for k in range(1, SLOTS):
        rank = rank + jnp.where((lane >= k) & (pltpu.roll(a, k, 1) == a), 1, 0)
    ay = (a // NC) % NY
    spot = ((a // (NY * NC)) * NC + a % NC) * (NY * SLOTS) + (ay % 2) * 32 + (ay // 2) * SLOTS + rank
    pick = onehot(iota((PACK, ROWS), 0) == spot)
    loads[3].wait()
    for t in range(4):
        cols = slice(256 * t, 256 * t + 256)
        got = jnp.dot(pick, tok[:, cols], preferred_element_type=F32)
        psend[:, :, cols] = got.reshape(GRP, PACK // GRP, 256).astype(BF16)

    loads[2].wait()
    pl.semaphore_wait(barrier, 2 + GRP - 1 + NZ - 1)

    def ring(ss, rs, to, step, s, f):
        i = (my + NY + step * s) % NY
        return pltpu.make_async_remote_copy(
            src_ref=maps.at[i, f], dst_ref=maps.at[i, f], send_sem=ss.at[PIECES * s + f], recv_sem=rs.at[PIECES * s + f],
            device_id={"rep": to}, device_id_type=MESH)

    hops = [(s, f) for s in range(3) for f in range(PIECES)]
    last_right = [(3, f) for f in range(PIECES // 2)]
    last_left = [(3, f) for f in range(PIECES // 2, PIECES)]
    to_right = {h: ring(s_yr, r_yr, rep_y(1), -1, *h) for h in hops + last_right}
    to_left = {h: ring(s_yl, r_yl, rep_y(NY - 1), 1, *h) for h in hops + last_left}
    for f in range(PIECES):
        to_right[0, f].start()
        to_left[0, f].start()

    def xcopy(k):
        h = grp(k)
        return pltpu.make_async_remote_copy(
            src_ref=psend.at[h], dst_ref=rrecv.at[mh], send_sem=s_x.at[k], recv_sem=r_x.at[k],
            device_id={"rep": rep_of(h, my)}, device_id_type=MESH)

    def run(make, what, count):
        def body(k, c):
            getattr(make(k), what)()
            return c
        lax.fori_loop(0, count - 1, body, 0)

    run(xcopy, "start", GRP)
    rrecv[mh] = psend[mh]

    loads[4].wait()
    for t in range(4):
        got = jnp.dot(tok[...], w[:, 256 * t:256 * t + 256], preferred_element_type=F32).astype(BF16)
        bsend[2 * t] = got[:, :PART]
        bsend[2 * t + 1] = got[:, PART:]

    def zcopy(src, dst, ss, rs):
        def make(k):
            return pltpu.make_async_remote_copy(
                src_ref=src(zp(k)), dst_ref=dst.at[z], send_sem=ss.at[k], recv_sem=rs.at[k],
                device_id={"tp": zp(k)}, device_id_type=MESH)
        return make

    bcopy = zcopy(lambda t: bsend.at[t], brecv, s_b, r_b)
    run(bcopy, "start", NZ)
    brecv[z] = bsend[z]

    loads[5].wait()
    for s, f in hops:
        for way in (to_right, to_left):
            way[s, f].wait_recv()
            if (s + 1, f) in way:
                way[s + 1, f].start()
    for h in last_right:
        to_right[h].wait_recv()
    for h in last_left:
        to_left[h].wait_recv()

    def mcopy(k):
        return pltpu.make_async_remote_copy(
            src_ref=ups.at[my], dst_ref=ups.at[my], send_sem=s_m.at[k], recv_sem=r_m.at[k],
            device_id={"rep": rep_y(far(k, NY))}, device_id_type=MESH)

    run(mcopy, "start", NY)
    run(xcopy, "wait_recv", GRP)

    r_all = rrecv[...].reshape(PACK, WIDTH)
    fold = jnp.zeros((PACK, PART), F32)
    row = iota((PACK, PART), 0)
    half = iota((PACK, PART), 1) // RANK
    mine = (row % 64) // 32 == half
    for t in range(2):
        d4 = maps[4 * t:4 * t + 4].reshape(4 * RANK, WIDTH)
        got = lax.dot_general(r_all, d4, (((1,), (1,)), ((), ())), preferred_element_type=F32)
        for i in range(2):
            keep = mine & ((row % 32) // SLOTS == 2 * t + i)
            fold = fold + jnp.where(keep, got[:, PART * i:PART * i + PART], 0.0)
    fold = fold.reshape(GRP, 2, 32, PART)
    csend[...] = fold[:, 0] + fold[:, 1]
    ccopy = zcopy(lambda t: csend.at[t], crecv, s_c, r_c)
    run(ccopy, "start", NZ)
    crecv[z] = csend[z]

    square = iota((ROWS, ROWS), 0) == iota((ROWS, ROWS), 1)
    spot_col = jnp.sum(jnp.where(square, spot.astype(F32), 0.0), axis=1, keepdims=True).astype(jnp.int32)
    back = onehot(iota((ROWS, PACK), 1) == spot_col)
    loads[1].wait()
    d_row = dest[...]
    d_col = jnp.sum(jnp.where(square, d_row.astype(F32), 0.0), axis=1, keepdims=True).astype(jnp.int32)
    earlier = (d_col == d_row) & (iota((ROWS, ROWS), 0) < iota((ROWS, ROWS), 1))
    slot = jnp.sum(jnp.where(earlier, 1.0, 0.0), axis=0, keepdims=True).astype(jnp.int32)
    place = onehot(iota((PACK, ROWS), 0) == d_row * SLOTS + slot)

    run(bcopy, "wait_recv", NZ)
    base = jnp.sum(brecv[...].astype(F32), axis=0)
    run(ccopy, "wait_recv", NZ)
    usend[...] = jnp.sum(crecv[...], axis=0).astype(BF16)
    ucopy = zcopy(lambda t: usend, urecv, s_u, r_u)
    run(ucopy, "start", NZ)
    urecv[z] = usend[...]
    run(ucopy, "wait_recv", NZ)

    run(mcopy, "wait_recv", NY)
    u = urecv[...].astype(F32).reshape(NZ, 4, SLOTS, PART)
    first = iota((NZ * SLOTS, PART), 1) < RANK
    for i in range(4):
        ui = u[:, i].reshape(NZ * SLOTS, PART)
        both = jnp.concatenate([jnp.where(first, ui, 0.0), jnp.where(first, 0.0, ui)], axis=0).astype(BF16)
        up2 = ups[2 * i:2 * i + 2].reshape(2 * RANK, PART)
        got = jnp.dot(both, up2, preferred_element_type=F32).astype(BF16)
        got = got.reshape(2, NZ, SLOTS, PART)
        for p in range(2):
            dsend[:, 32 * p + SLOTS * i:32 * p + SLOTS * i + SLOTS] = got[p]

    def dcopy(k):
        h = grp(k)
        return pltpu.make_async_remote_copy(
            src_ref=dsend.at[h], dst_ref=drecv.at[mh], send_sem=s_d.at[k], recv_sem=r_d.at[k],
            device_id={"rep": rep_of(h, my)}, device_id_type=MESH)

    run(dcopy, "start", GRP)
    drecv[mh] = dsend[mh]
    run(dcopy, "wait_recv", GRP)

    delta = jnp.dot(back, drecv[...].reshape(PACK, PART), preferred_element_type=F32)
    keyrow = (base + 2.0 * delta).astype(BF16)
    got = jnp.dot(place, keyrow, preferred_element_type=F32)
    osend[...] = got.reshape(REP, SLOTS, PART).astype(BF16)

    def ocopy(k):
        to = anyone(k)
        return pltpu.make_async_remote_copy(
            src_ref=osend.at[to], dst_ref=orecv.at[me], send_sem=s_o.at[k], recv_sem=r_o.at[k],
            device_id={"rep": to}, device_id_type=MESH)

    run(ocopy, "start", REP)
    orecv[me] = osend[me]
    for way in (to_right, to_left):
        for c in way.values():
            c.wait_send()
    run(mcopy, "wait_send", NY)
    run(xcopy, "wait_send", GRP)
    run(bcopy, "wait_send", NZ)
    run(ccopy, "wait_send", NZ)
    run(ucopy, "wait_send", NZ)
    run(dcopy, "wait_send", GRP)
    run(ocopy, "wait_recv", REP)
    run(ocopy, "wait_send", REP)
    out[...] = orecv[...]


def per_device(tokens, key_weight_base, adapter_down_maps, adapter_up_maps, adapter_index, plan):
    vm = pl.BlockSpec(memory_space=pltpu.VMEM)
    dma = pltpu.SemaphoreType.DMA
    got = pl.pallas_call(
        kernel,
        out_shape=jax.ShapeDtypeStruct((REP, SLOTS, PART), BF16),
        in_specs=[pl.BlockSpec(memory_space=pl.ANY)] * 6,
        out_specs=vm,
        scratch_shapes=[
            pltpu.VMEM((ROWS, WIDTH), BF16),
            pltpu.VMEM((WIDTH, KEYS), BF16),
            pltpu.VMEM((1, ROWS), jnp.int32),
            pltpu.VMEM((1, ROWS), jnp.int32),
            pltpu.VMEM((GRP, PACK // GRP, WIDTH), BF16),
            pltpu.VMEM((GRP, PACK // GRP, WIDTH), BF16),
            pltpu.VMEM((NY, PIECES, RANK // PIECES, WIDTH), BF16),
            pltpu.VMEM((NY, RANK, PART), BF16),
            pltpu.VMEM((NZ, ROWS, PART), BF16),
            pltpu.VMEM((NZ, ROWS, PART), BF16),
            pltpu.VMEM((GRP, 32, PART), F32),
            pltpu.VMEM((NZ, 32, PART), F32),
            pltpu.VMEM((32, PART), BF16),
            pltpu.VMEM((NZ, 32, PART), BF16),
            pltpu.VMEM((GRP, PACK // GRP, PART), BF16),
            pltpu.VMEM((GRP, PACK // GRP, PART), BF16),
            pltpu.VMEM((REP, SLOTS, PART), BF16),
            pltpu.VMEM((REP, SLOTS, PART), BF16),
            dma((6,)), dma((NY,)), dma((NY,)), dma((GRP,)), dma((GRP,)),
            dma((4 * PIECES,)), dma((4 * PIECES,)), dma((4 * PIECES,)), dma((4 * PIECES,)),
            dma((NZ,)), dma((NZ,)),
            dma((NZ,)), dma((NZ,)),
            dma((NZ,)), dma((NZ,)),
            dma((GRP,)), dma((GRP,)),
            dma((REP,)), dma((REP,)),
        ],
        compiler_params=pltpu.CompilerParams(collective_id=0, has_side_effects=True),
        name="keys",
    )(
        tokens, key_weight_base, adapter_down_maps.reshape(WIDTH, RANK).T.reshape(PIECES, RANK // PIECES, WIDTH),
        adapter_up_maps.reshape(RANK, PART), adapter_index, plan.reshape(1, ROWS),
    )
    return got.reshape(PACK, PART)


def solution(mesh):
    placed = (
        P("rep", "tp"),
        P("tp", None),
        P("rep", "tp", None),
        P("rep", None, "tp"),
        P("rep", None),
        P("rep", None),
    )
    return jax.shard_map(
        per_device, mesh=mesh, in_specs=placed, out_specs=P("rep", "tp"), check_vma=False
    )
```
